512 devices in a mesh: ka: 64 (over z_lo, x, core), mu: 8 (over y, z_hi).
Axes of the slice: x: 4, y: 4, z: 16 (z_hi: 2, z_lo: 8; z = z_hi * 8 + z_lo), core: 2. Of those that a mesh axis runs over, the one named last changes fastest.
Arguments:
- vectors: float32 [3, 64, 4096], P(None, 'ka', 'mu'), may hold values from -6 to 6
- phi_val: bfloat16 [64, 64, 2048], P('ka', None, 'mu'), may hold values from -6 to 6
- phi_con: bfloat16 [64, 64, 2048], P('ka', None, 'mu'), may hold values from -6 to 6
- screened: bfloat16 [4, 2048, 2048], P(None, 'mu'), may hold values from -4.5776367e-05 to 4.5776367e-05
- partner: int32 [64, 4], P('ka'), may hold values from 0 to 63, as said below
Outputs:
- result: float32 [3, 64, 4096], P(None, 'ka', 'mu')
The draws below stay inside these ranges and needn't reach their ends.
Inputs may be any that keep to these rules, and one draw needn't show every extreme that they name: With s = (1, -1, 2, -2) for offsets 0 to 3, partner[k, o] = (k - s[o]) modulo 64; each ka index j holds exactly one k-point, k-point j.
All inputs are finite; a program needn't handle non-finite values.
Results may differ from the reference program's by a relative error of at most 0.0058.
Values may be sent and summed in bfloat16 or wider, within the bound.
A program may use at most 64 MiB of HBM per device.

```python
import jax
import jax.numpy as jnp
from jax import lax

NV = 64
NC = 64
NMU = 2048
NVEC = 3
NOFF = 4
KD = 1
NK = 64
PAIRS = 4096


cycle_steps = (1, -1, 2, -2)


def draw_partner(key, part):
    blocks = NK // KD
    key_list = jax.random.split(key, blocks * NOFF)
    slot_table = jax.vmap(lambda single: jax.random.permutation(single, KD))(key_list)
    slot_table = jnp.transpose(slot_table.reshape(blocks, NOFF, KD), (0, 2, 1)).astype(jnp.int32)
    home_block = jnp.arange(blocks, dtype=jnp.int32)[:, None, None]
    cycle_shift = jnp.array(cycle_steps, jnp.int32)[None, None, :]
    source = jnp.mod(home_block - cycle_shift, blocks)
    return (source * KD + slot_table).reshape(NK, NOFF)


def block_scale(own_key, dims, cuts, low, largest):
    def one(dim, shards_of):
        steps = jax.random.uniform(jax.random.fold_in(jax.random.fold_in(own_key, 6), dim), (shards_of,), jnp.float32, low / len(cuts), largest / len(cuts))
        return jnp.repeat(jnp.exp(steps), dims[dim] // shards_of).reshape((-1,) + (1,) * (len(dims) - dim - 1))

    factor_of = one(*cuts[0])
    for cut in cuts[1:]:
        factor_of = factor_of * one(*cut)
    return factor_of


def centred(rng, shape, spread, reach, pieces=(), kind=jnp.bfloat16):
    factor_of = block_scale(rng, shape, pieces, -0.22, 0.18) if pieces else 1.0
    values = jax.random.normal(rng, shape, jnp.float32) * spread * factor_of
    return jnp.minimum(jnp.maximum(values, -reach), reach).astype(kind)


def setup_inputs(seed: int = 0) -> dict:
    splits = jax.random.split(jax.random.key(seed), 6)
    vectors = centred(splits[0], (NVEC, NK, PAIRS), 1.0, 6.0, ((1, 64), (2, 8)), jnp.float32)
    phi_val = centred(splits[1], (NK, NV, NMU), 1.0, 6.0, ((0, 64), (2, 8)))
    phi_con = centred(splits[2], (NK, NC, NMU), 1.0, 6.0, ((0, 64), (2, 8)))
    screened = centred(splits[3], (NOFF, NMU, NMU), (1.0 / (NMU * NV)), 4.57763671875e-05, ((1, 8),))
    partner = draw_partner(jax.random.fold_in(splits[5], 71), 0)
    return {"vectors": vectors, "phi_val": phi_val, "phi_con": phi_con, "screened": screened, "partner": partner}


def reference(vectors, phi_val, phi_con, screened, partner):
    vec_coded = vectors.astype(jnp.bfloat16).reshape(NVEC, NK, NV, NC)

    def one_point(point_item):
        val_own, con_own, partners = point_item
        running_sum = jnp.zeros((NVEC, NV, NC), jnp.float32)
        for offset in range(NOFF):
            source = partners[offset]
            val_far = lax.dynamic_index_in_dim(phi_val, source, 0, keepdims=False)
            con_far = lax.dynamic_index_in_dim(phi_con, source, 0, keepdims=False)
            vec_far = lax.dynamic_index_in_dim(vec_coded, source, 1, keepdims=False)
            blended = jnp.einsum('svc,cn->svn', vec_far.astype(jnp.float32), con_far.astype(jnp.float32)).astype(jnp.bfloat16)
            paired = jnp.einsum('vm,svn->smn', val_far.astype(jnp.float32), blended.astype(jnp.float32))
            weighted = (screened[offset].astype(jnp.float32)[None] * paired).astype(jnp.bfloat16)
            folded = jnp.einsum('smn,cn->smc', weighted.astype(jnp.float32), con_own.astype(jnp.float32)).astype(jnp.bfloat16)
            running_sum = running_sum + jnp.einsum('vm,smc->svc', val_own.astype(jnp.float32), folded.astype(jnp.float32))
        return running_sum

    gathered = lax.map(one_point, (phi_val, phi_con, partner))
    return jnp.transpose(gathered, (1, 0, 2, 3)).reshape(NVEC, NK, NV * NC)
```

```python
import functools

import jax
import jax.numpy as jnp
from jax import lax
from jax.experimental import pallas as pl
from jax.experimental.pallas import tpu as pltpu
from jax.sharding import PartitionSpec as P

MESH = pl.DeviceIdType.MESH
STEPS = (1, -1, 2, -2)
F32 = jnp.float32
BF16 = jnp.bfloat16


def kernel(
    vec_hbm, val_hbm, con_hbm, scr_hbm, out_ref,
    vec, xbuf, xall, xpart, con_own, con_part, val_own, val_part, scr, yv, fold, fcat, rbuf, rin,
    load_sem, send_sem, rx, rxp, rval, rnear, rfar, rp, rout,
):
    nk = lax.axis_size("ka")
    nmu = lax.axis_size("mu")
    k = lax.axis_index("ka")
    mu = lax.axis_index("mu")
    y, zh = mu // 2, mu % 2

    def wrapped(s):
        whole = (k + s + nk) // nk
        return whole - 1 if s > 0 else 1 - whole

    def ka_of(s):
        return lax.rem(k + s + nk, nk)

    loads = [
        pltpu.make_async_copy(vec_hbm, vec, load_sem.at[0]),
        pltpu.make_async_copy(con_hbm.at[0], con_own.at[zh, y], load_sem.at[1]),
        pltpu.make_async_copy(val_hbm.at[0], val_own, load_sem.at[2]),
    ] + [pltpu.make_async_copy(scr_hbm.at[o], scr.at[o], load_sem.at[3 + o]) for o in range(4)]

    barrier = pltpu.get_barrier_semaphore()
    for d in range(1, nmu):
        pl.semaphore_signal(barrier, inc=1, device_id={"mu": lax.rem(mu + d, nmu)}, device_id_type=MESH)
    for s in STEPS:
        pl.semaphore_signal(barrier, inc=1, device_id={"ka": ka_of(s)}, device_id_type=MESH)
        pl.semaphore_signal(
            barrier, inc=1, device_id={"ka": ka_of(s), "mu": 2 * y + lax.rem(zh + wrapped(s), 2)}, device_id_type=MESH
        )
    for load in loads:
        load.start()
    loads[0].wait()
    xbuf[...] = jnp.zeros_like(xbuf)
    for s in range(3):
        for r in range(8):
            xbuf[r : r + 1, s * 64 : (s + 1) * 64] = vec[s, :, r * 64 : (r + 1) * 64]
    xall[mu] = xbuf[...].astype(BF16)
    loads[1].wait()
    loads[2].wait()
    pl.semaphore_wait(barrier, nmu - 1 + 8)

    sent = []

    def send(src, dst, recv, device):
        copy = pltpu.make_async_remote_copy(
            src_ref=src, dst_ref=dst, send_sem=send_sem.at[len(sent)], recv_sem=recv,
            device_id=device, device_id_type=MESH,
        )
        copy.start()
        sent.append(copy)

    def arrived(ref, recv):
        pltpu.make_async_remote_copy(
            src_ref=ref, dst_ref=ref, send_sem=send_sem.at[0], recv_sem=recv,
            device_id={"mu": lax.rem(mu + 1, nmu)}, device_id_type=MESH,
        ).wait_recv()

    def to_partners_near(yy):
        for o, s in enumerate(STEPS):
            src = con_own.at[zh, yy]
            send(src, con_part.at[o, zh, yy], rp.at[0, o, yy], {"ka": ka_of(s)})

    def to_partners_far(yy):
        for o, s in enumerate(STEPS):
            w = wrapped(s)
            half = lax.rem(zh + 1 + w, 2)
            send(
                con_own.at[half, yy], con_part.at[o, half, yy], rp.at[1, o, yy],
                {"ka": ka_of(s), "mu": 2 * y + lax.rem(zh + w, 2)},
            )

    zo = 1 - zh
    for d in range(1, nmu):
        peer = lax.rem(mu + d, nmu)
        send(xall.at[mu], xall.at[mu], rx.at[mu], {"mu": peer})
    send(con_own.at[zh, y], con_own.at[zh, y], rfar.at[y], {"mu": 2 * y + zo})
    for d in range(1, 4):
        send(con_own.at[zh, y], con_own.at[zh, y], rnear.at[y], {"mu": 2 * lax.rem(y + d, 4) + zh})
    for o, s in enumerate(STEPS):
        send(val_own, val_part.at[o], rval.at[o], {"ka": ka_of(s)})
    to_partners_near(y)
    for d in (1, 3, 2):
        yy = lax.rem(y + d, 4)
        arrived(con_own.at[zh, yy], rnear.at[yy])
        to_partners_near(yy)
    for d in range(1, nmu):
        peer = lax.rem(mu + d, nmu)
        arrived(xall.at[peer], rx.at[peer])
    for o, s in enumerate(STEPS):
        send(xall, xpart.at[o], rxp.at[o], {"ka": ka_of(s), "mu": 2 * y + lax.rem(zh + wrapped(s), 2)})
    arrived(con_own.at[zo, y], rfar.at[y])
    for d in range(1, 4):
        send(con_own.at[zo, y], con_own.at[zo, y], rfar.at[y], {"mu": 2 * lax.rem(y + d, 4) + zh})
    to_partners_far(y)
    for d in (1, 3, 2):
        yy = lax.rem(y + d, 4)
        arrived(con_own.at[zo, yy], rfar.at[yy])
        to_partners_far(yy)

    for o in range(4):
        arrived(xpart.at[o], rxp.at[o])
        arrived(val_part.at[o], rval.at[o])
        x = xpart[o].astype(F32).reshape(64, 256).astype(BF16)
        for s in range(3):
            part = lax.dot_general(
                val_part[o], x[:, s * 64 : (s + 1) * 64], (((0,), (0,)), ((), ())), preferred_element_type=F32
            )
            yv[o, s * 256 : (s + 1) * 256, :] = part.astype(BF16)
    fold[...] = jnp.zeros_like(fold)
    for load in loads[3:]:
        load.wait()

    def block(i, carry):
        phase = i // 4
        half = lax.rem(zh + phase, 2)
        yy = lax.rem(y + i, 4)
        for o in range(4):
            arrived(con_part.at[o, half, yy], rp.at[phase, o, yy])
        columns = pl.ds(pl.multiple_of((2 * yy + half) * 256, 256), 256)
        for s in range(3):
            rows = slice(s * 256, (s + 1) * 256)
            total = None
            for o in range(4):
                paired = jnp.dot(yv[o, rows, :], con_part[o, half, yy], preferred_element_type=F32)
                term = scr[o, :, columns].astype(F32) * paired
                total = term if total is None else total + term
            fold[rows, :] += lax.dot_general(
                total.astype(BF16), con_own[half, yy], (((1,), (1,)), ((), ())), preferred_element_type=F32
            )
        return carry

    lax.fori_loop(0, 8, block, 0)

    for s in range(3):
        fcat[:, s * 64 : (s + 1) * 64] = fold[s * 256 : (s + 1) * 256, :].astype(BF16)
    result = jnp.dot(val_own[...], fcat[...], preferred_element_type=F32)
    for j in range(8):
        rbuf[j] = result[j * 8 : (j + 1) * 8, :].astype(BF16)
    for d in range(1, nmu):
        peer = lax.rem(mu + d, nmu)
        send(rbuf.at[peer], rin.at[mu], rout.at[mu], {"mu": peer})
    total = rbuf[mu].astype(F32)
    for d in range(1, nmu):
        peer = lax.rem(mu + d, nmu)
        arrived(rin.at[peer], rout.at[peer])
        total = total + rin[peer].astype(F32)
    out_ref[...] = total
    for copy in sent:
        copy.wait_send()


def local(vectors, phi_val, phi_con, screened, partner):
    anyspace = pl.BlockSpec(memory_space=pl.ANY)
    dma = pltpu.SemaphoreType.DMA
    out = pl.pallas_call(
        kernel,
        out_shape=jax.ShapeDtypeStruct((8, 256), F32),
        in_specs=[anyspace] * 4,
        out_specs=pl.BlockSpec(memory_space=pltpu.VMEM),
        scratch_shapes=[
            pltpu.VMEM((3, 1, 512), F32),
            pltpu.VMEM((8, 256), F32),
            pltpu.VMEM((8, 8, 256), BF16),
            pltpu.VMEM((4, 8, 8, 256), BF16),
            pltpu.VMEM((2, 4, 64, 256), BF16),
            pltpu.VMEM((4, 2, 4, 64, 256), BF16),
            pltpu.VMEM((64, 256), BF16),
            pltpu.VMEM((4, 64, 256), BF16),
            pltpu.VMEM((4, 256, 2048), BF16),
            pltpu.VMEM((4, 768, 64), BF16),
            pltpu.VMEM((768, 64), F32),
            pltpu.VMEM((256, 256), BF16),
            pltpu.VMEM((8, 8, 256), BF16),
            pltpu.VMEM((8, 8, 256), BF16),
            dma((7,)),
            dma((64,)),
            dma((8,)),
            dma((4,)),
            dma((4,)),
            dma((4,)),
            dma((4,)),
            dma((2, 4, 4)),
            dma((8,)),
        ],
        compiler_params=pltpu.CompilerParams(collective_id=0, has_side_effects=True),
        name="isdf_direct",
    )(vectors, phi_val, phi_con, screened)
    return out[:, :192].reshape(8, 3, 64).transpose(1, 0, 2).reshape(3, 1, 512)


def solution(mesh):
    placed = (
        P(None, "ka", "mu"),
        P("ka", None, "mu"),
        P("ka", None, "mu"),
        P(None, "mu", None),
        P("ka", None),
    )
    return jax.shard_map(
        local, mesh=mesh, in_specs=placed, out_specs=P(None, "ka", "mu"), check_vma=False
    )
```

```python
import functools

import jax
import jax.numpy as jnp
from jax import lax
from jax.experimental import pallas as pl
from jax.experimental.pallas import tpu as pltpu
from jax.sharding import PartitionSpec as P

MESH = pl.DeviceIdType.MESH
STEPS = (1, -1, 2, -2)
F32 = jnp.float32
BF16 = jnp.bfloat16


def kernel(
    vec_hbm, val_hbm, con_hbm, scr_hbm, out_ref,
    vec, xbuf, xall, xpart, con_own, con_part, val_own, val_part, scr, yv, val_t, acc, wsum, foldt, fcat, rbuf, rin,
    load_sem, send_sem, rx, rxp, rval, rnear, rfar, rp, rout,
):
    nk = lax.axis_size("ka")
    nmu = lax.axis_size("mu")
    k = lax.axis_index("ka")
    mu = lax.axis_index("mu")
    y, zh = mu // 2, mu % 2

    def wrapped(s):
        whole = (k + s + nk) // nk
        return whole - 1 if s > 0 else 1 - whole

    def ka_of(s):
        return lax.rem(k + s + nk, nk)

    loads = [
        pltpu.make_async_copy(vec_hbm, vec, load_sem.at[0]),
        pltpu.make_async_copy(con_hbm.at[0], con_own.at[zh, y], load_sem.at[1]),
        pltpu.make_async_copy(val_hbm.at[0], val_own, load_sem.at[2]),
    ] + [pltpu.make_async_copy(scr_hbm.at[o], scr.at[o], load_sem.at[3 + o]) for o in range(4)]

    barrier = pltpu.get_barrier_semaphore()
    for d in range(1, nmu):
        pl.semaphore_signal(barrier, inc=1, device_id={"mu": lax.rem(mu + d, nmu)}, device_id_type=MESH)
    for s in STEPS:
        pl.semaphore_signal(barrier, inc=1, device_id={"ka": ka_of(s)}, device_id_type=MESH)
        pl.semaphore_signal(
            barrier, inc=1, device_id={"ka": ka_of(s), "mu": 2 * y + lax.rem(zh + wrapped(s), 2)}, device_id_type=MESH
        )
    for load in loads:
        load.start()
    loads[0].wait()
    xbuf[...] = jnp.zeros_like(xbuf)
    for s in range(3):
        for r in range(8):
            xbuf[r : r + 1, s * 64 : (s + 1) * 64] = vec[s, :, r * 64 : (r + 1) * 64]
    xall[mu] = xbuf[...].astype(BF16)
    rbuf[...] = jnp.zeros_like(rbuf)
    loads[1].wait()
    loads[2].wait()
    pl.semaphore_wait(barrier, nmu - 1 + 8)

    sent = []

    def send(src, dst, recv, device):
        copy = pltpu.make_async_remote_copy(
            src_ref=src, dst_ref=dst, send_sem=send_sem.at[len(sent)], recv_sem=recv,
            device_id=device, device_id_type=MESH,
        )
        copy.start()
        sent.append(copy)

    def arrived(ref, recv):
        pltpu.make_async_remote_copy(
            src_ref=ref, dst_ref=ref, send_sem=send_sem.at[0], recv_sem=recv,
            device_id={"mu": lax.rem(mu + 1, nmu)}, device_id_type=MESH,
        ).wait_recv()

    def to_partners_near(yy):
        for o, s in enumerate(STEPS):
            src = con_own.at[zh, yy]
            send(src, con_part.at[o, zh, yy], rp.at[0, o, yy], {"ka": ka_of(s)})

    def to_partners_far(yy):
        for o, s in enumerate(STEPS):
            w = wrapped(s)
            half = lax.rem(zh + 1 + w, 2)
            send(
                con_own.at[half, yy], con_part.at[o, half, yy], rp.at[1, o, yy],
                {"ka": ka_of(s), "mu": 2 * y + lax.rem(zh + w, 2)},
            )

    zo = 1 - zh
    for d in range(1, nmu):
        peer = lax.rem(mu + d, nmu)
        send(xall.at[mu], xall.at[mu], rx.at[mu], {"mu": peer})
    send(con_own.at[zh, y], con_own.at[zh, y], rfar.at[y], {"mu": 2 * y + zo})
    for d in range(1, 4):
        send(con_own.at[zh, y], con_own.at[zh, y], rnear.at[y], {"mu": 2 * lax.rem(y + d, 4) + zh})
    for o, s in enumerate(STEPS):
        send(val_own, val_part.at[o], rval.at[o], {"ka": ka_of(s)})
    to_partners_near(y)
    for d in (1, 3, 2):
        yy = lax.rem(y + d, 4)
        arrived(con_own.at[zh, yy], rnear.at[yy])
        to_partners_near(yy)
    for d in range(1, nmu):
        peer = lax.rem(mu + d, nmu)
        arrived(xall.at[peer], rx.at[peer])
    for o, s in enumerate(STEPS):
        send(xall, xpart.at[o], rxp.at[o], {"ka": ka_of(s), "mu": 2 * y + lax.rem(zh + wrapped(s), 2)})
    arrived(con_own.at[zo, y], rfar.at[y])
    for d in range(1, 4):
        send(con_own.at[zo, y], con_own.at[zo, y], rfar.at[y], {"mu": 2 * lax.rem(y + d, 4) + zh})
    to_partners_far(y)
    for d in (1, 3, 2):
        yy = lax.rem(y + d, 4)
        arrived(con_own.at[zo, yy], rfar.at[yy])
        to_partners_far(yy)

    for o in range(4):
        arrived(val_part.at[o], rval.at[o])
        val_t[o] = val_part[o].astype(F32).T.astype(BF16)
    foldt[...] = jnp.zeros_like(foldt)
    for o in range(4):
        arrived(xpart.at[o], rxp.at[o])
        x = xpart[o].astype(F32).reshape(64, 256).astype(BF16)
        mixed = jnp.dot(val_t[o], x, preferred_element_type=F32).astype(BF16)
        for s in range(3):
            yv[o, s * 256 : (s + 1) * 256, :] = mixed[:, s * 64 : (s + 1) * 64]
    for load in loads[3:]:
        load.wait()

    def block(i, carry):
        phase = i // 4
        half = lax.rem(zh + phase, 2)
        turn = lax.rem(i, 4)
        yy = lax.rem(y + turn + (turn // 2) * (1 - 2 * (turn % 2)), 4)
        for o in range(4):
            arrived(con_part.at[o, half, yy], rp.at[phase, o, yy])
        columns = pl.ds(pl.multiple_of((2 * yy + half) * 256, 256), 256)
        for o in range(4):
            weight = scr[o, :, columns].astype(F32)
            for s in range(3):
                rows = slice(s * 256, (s + 1) * 256)
                term = weight * jnp.dot(yv[o, rows, :], con_part[o, half, yy], preferred_element_type=F32)
                if o == 0:
                    acc[rows, :] = term
                elif o < 3:
                    acc[rows, :] += term
                else:
                    wsum[rows, :] = (acc[rows, :] + term).astype(BF16)
        foldt[...] += lax.dot_general(
            con_own[half, yy], wsum[...], (((1,), (1,)), ((), ())), preferred_element_type=F32
        )
        return carry

    lax.fori_loop(0, 8, block, 0)

    for s in range(3):
        fcat[s * 64 : (s + 1) * 64, :] = foldt[:, s * 256 : (s + 1) * 256].astype(BF16)
    result = lax.dot_general(
        val_own[...], fcat[...], (((1,), (1,)), ((), ())), preferred_element_type=F32
    )
    for j in range(8):
        rbuf[j, :, 0:192] = result[j * 8 : (j + 1) * 8, :].astype(BF16)
    for d in range(1, nmu):
        peer = lax.rem(mu + d, nmu)
        send(rbuf.at[peer], rin.at[mu], rout.at[mu], {"mu": peer})
    total = rbuf[mu].astype(F32)
    for d in range(1, nmu):
        peer = lax.rem(mu + d, nmu)
        arrived(rin.at[peer], rout.at[peer])
        total = total + rin[peer].astype(F32)
    for s in range(3):
        out_ref[s] = total[:, s * 64 : (s + 1) * 64]
    for copy in sent:
        copy.wait_send()


def local(vectors, phi_val, phi_con, screened, partner):
    anyspace = pl.BlockSpec(memory_space=pl.ANY)
    dma = pltpu.SemaphoreType.DMA
    out = pl.pallas_call(
        kernel,
        out_shape=jax.ShapeDtypeStruct((3, 8, 64), F32),
        in_specs=[anyspace] * 4,
        out_specs=pl.BlockSpec(memory_space=pltpu.VMEM),
        scratch_shapes=[
            pltpu.VMEM((3, 1, 512), F32),
            pltpu.VMEM((8, 256), F32),
            pltpu.VMEM((8, 8, 256), BF16),
            pltpu.VMEM((4, 8, 8, 256), BF16),
            pltpu.VMEM((2, 4, 64, 256), BF16),
            pltpu.VMEM((4, 2, 4, 64, 256), BF16),
            pltpu.VMEM((64, 256), BF16),
            pltpu.VMEM((4, 64, 256), BF16),
            pltpu.VMEM((4, 256, 2048), BF16),
            pltpu.VMEM((4, 768, 64), BF16),
            pltpu.VMEM((4, 256, 64), BF16),
            pltpu.VMEM((768, 256), F32),
            pltpu.VMEM((768, 256), BF16),
            pltpu.VMEM((64, 768), F32),
            pltpu.VMEM((192, 256), BF16),
            pltpu.VMEM((8, 8, 256), BF16),
            pltpu.VMEM((8, 8, 256), BF16),
            dma((7,)),
            dma((64,)),
            dma((8,)),
            dma((4,)),
            dma((4,)),
            dma((4,)),
            dma((4,)),
            dma((2, 4, 4)),
            dma((8,)),
        ],
        compiler_params=pltpu.CompilerParams(collective_id=0, has_side_effects=True),
        name="isdf_direct",
    )(vectors, phi_val, phi_con, screened)
    return out.reshape(3, 1, 512)


def solution(mesh):
    placed = (
        P(None, "ka", "mu"),
        P("ka", None, "mu"),
        P("ka", None, "mu"),
        P(None, "mu", None),
        P("ka", None),
    )
    return jax.shard_map(
        local, mesh=mesh, in_specs=placed, out_specs=P(None, "ka", "mu"), check_vma=False
    )
```

```python
import functools

import jax
import jax.numpy as jnp
from jax import lax
from jax.experimental import pallas as pl
from jax.experimental.pallas import tpu as pltpu
from jax.sharding import PartitionSpec as P

MESH = pl.DeviceIdType.MESH
STEPS = (1, -1, 2, -2)
F32 = jnp.float32
BF16 = jnp.bfloat16


def kernel(
    vec_hbm, val_hbm, con_hbm, scr_hbm, out_ref,
    vec, xbuf, xall, xpart, con_own, con_part, val_own, val_part, scr, yv, val_t, acc, wsum, foldt, fcat, rbuf, rin,
    load_sem, send_sem, rx, rxp, rval, rnear, rfar, rp, rout,
):
    nk = lax.axis_size("ka")
    nmu = lax.axis_size("mu")
    k = lax.axis_index("ka")
    mu = lax.axis_index("mu")
    y, zh = mu // 2, mu % 2

    def wrapped(s):
        whole = (k + s + nk) // nk
        return whole - 1 if s > 0 else 1 - whole

    def ka_of(s):
        return lax.rem(k + s + nk, nk)

    loads = [
        pltpu.make_async_copy(vec_hbm, vec, load_sem.at[0]),
        pltpu.make_async_copy(con_hbm.at[0], con_own.at[zh, y], load_sem.at[1]),
        pltpu.make_async_copy(val_hbm.at[0], val_own, load_sem.at[2]),
    ] + [pltpu.make_async_copy(scr_hbm.at[o], scr.at[o], load_sem.at[3 + o]) for o in range(4)]

    barrier = pltpu.get_barrier_semaphore()
    def greet(device):
        pl.semaphore_signal(barrier, inc=1, device_id=device, device_id_type=MESH)

    def near_half(s):
        return lax.rem(zh + wrapped(s), 2)

    greet({"mu": 2 * y + 1 - zh})
    for d in range(1, 4):
        greet({"mu": 2 * lax.rem(y + d, 4) + zh})
    for s in STEPS:
        greet({"ka": ka_of(s)})
        for yy in range(4):
            greet({"ka": ka_of(s), "mu": 2 * yy + near_half(s)})
    for load in loads:
        load.start()
    loads[0].wait()
    xbuf[...] = jnp.zeros_like(xbuf)
    for s in range(3):
        for r in range(8):
            xbuf[r : r + 1, s * 64 : (s + 1) * 64] = vec[s, :, r * 64 : (r + 1) * 64]
    xall[mu] = xbuf[...].astype(BF16)
    rbuf[...] = jnp.zeros_like(rbuf)
    loads[1].wait()
    loads[2].wait()
    pl.semaphore_wait(barrier, 24)

    sent = []

    def send(src, dst, recv, device):
        copy = pltpu.make_async_remote_copy(
            src_ref=src, dst_ref=dst, send_sem=send_sem.at[len(sent)], recv_sem=recv,
            device_id=device, device_id_type=MESH,
        )
        copy.start()
        sent.append(copy)

    def arrived(ref, recv):
        pltpu.make_async_remote_copy(
            src_ref=ref, dst_ref=ref, send_sem=send_sem.at[0], recv_sem=recv,
            device_id={"mu": lax.rem(mu + 1, nmu)}, device_id_type=MESH,
        ).wait_recv()

    def to_partners_near(yy):
        for o, s in enumerate(STEPS):
            src = con_own.at[zh, yy]
            send(src, con_part.at[o, zh, yy], rp.at[0, o, yy], {"ka": ka_of(s)})

    def to_partners_far(yy):
        for o, s in enumerate(STEPS):
            w = wrapped(s)
            half = lax.rem(zh + 1 + w, 2)
            send(
                con_own.at[half, yy], con_part.at[o, half, yy], rp.at[1, o, yy],
                {"ka": ka_of(s), "mu": 2 * y + lax.rem(zh + w, 2)},
            )

    zo = 1 - zh
    def x_to_partners(m):
        for d in range(4):
            for o, s in enumerate(STEPS):
                send(
                    xall.at[m], xpart.at[o, m], rxp.at[o, m],
                    {"ka": ka_of(s), "mu": 2 * lax.rem(y + d, 4) + near_half(s)},
                )

    send(xall.at[mu], xall.at[mu], rx.at[mu], {"mu": 2 * y + zo})
    send(con_own.at[zh, y], con_own.at[zh, y], rfar.at[y], {"mu": 2 * y + zo})
    for d in range(1, 4):
        send(con_own.at[zh, y], con_own.at[zh, y], rnear.at[y], {"mu": 2 * lax.rem(y + d, 4) + zh})
    for o, s in enumerate(STEPS):
        send(val_own, val_part.at[o], rval.at[o], {"ka": ka_of(s)})
    to_partners_near(y)
    for d in (1, 3, 2):
        yy = lax.rem(y + d, 4)
        arrived(con_own.at[zh, yy], rnear.at[yy])
        to_partners_near(yy)
    x_to_partners(mu)
    far = 2 * y + zo
    arrived(xall.at[far], rx.at[far])
    x_to_partners(far)
    arrived(con_own.at[zo, y], rfar.at[y])
    for d in range(1, 4):
        send(con_own.at[zo, y], con_own.at[zo, y], rfar.at[y], {"mu": 2 * lax.rem(y + d, 4) + zh})
    to_partners_far(y)
    for d in (1, 3, 2):
        yy = lax.rem(y + d, 4)
        arrived(con_own.at[zo, yy], rfar.at[yy])
        to_partners_far(yy)

    for o in range(4):
        arrived(val_part.at[o], rval.at[o])
        val_t[o] = val_part[o].astype(F32).T.astype(BF16)
    foldt[...] = jnp.zeros_like(foldt)
    for o in range(4):
        for m in range(8):
            arrived(xpart.at[o, m], rxp.at[o, m])
        x = xpart[o].astype(F32).reshape(64, 256).astype(BF16)
        mixed = jnp.dot(val_t[o], x, preferred_element_type=F32).astype(BF16)
        for s in range(3):
            yv[o, s * 256 : (s + 1) * 256, :] = mixed[:, s * 64 : (s + 1) * 64]
    for load in loads[3:]:
        load.wait()

    def block(i, carry):
        phase = i // 4
        half = lax.rem(zh + phase, 2)
        turn = lax.rem(i, 4)
        yy = lax.rem(y + turn + (turn // 2) * (1 - 2 * (turn % 2)), 4)
        for o in range(4):
            arrived(con_part.at[o, half, yy], rp.at[phase, o, yy])
        columns = pl.ds(pl.multiple_of((2 * yy + half) * 256, 256), 256)
        for o in range(4):
            weight = scr[o, :, columns].astype(F32)
            for s in range(3):
                rows = slice(s * 256, (s + 1) * 256)
                term = weight * jnp.dot(yv[o, rows, :], con_part[o, half, yy], preferred_element_type=F32)
                if o == 0:
                    acc[rows, :] = term
                elif o < 3:
                    acc[rows, :] += term
                else:
                    wsum[rows, :] = (acc[rows, :] + term).astype(BF16)
        foldt[...] += lax.dot_general(
            con_own[half, yy], wsum[...], (((1,), (1,)), ((), ())), preferred_element_type=F32
        )
        return carry

    lax.fori_loop(0, 8, block, 0)

    for s in range(3):
        fcat[s * 64 : (s + 1) * 64, :] = foldt[:, s * 256 : (s + 1) * 256].astype(BF16)
    result = lax.dot_general(
        val_own[...], fcat[...], (((1,), (1,)), ((), ())), preferred_element_type=F32
    )
    for j in range(8):
        rbuf[j, :, 0:192] = result[j * 8 : (j + 1) * 8, :].astype(BF16)
    for d in range(1, nmu):
        peer = lax.rem(mu + d, nmu)
        send(rbuf.at[peer], rin.at[mu], rout.at[mu], {"mu": peer})
    total = rbuf[mu].astype(F32)
    for d in range(1, nmu):
        peer = lax.rem(mu + d, nmu)
        arrived(rin.at[peer], rout.at[peer])
        total = total + rin[peer].astype(F32)
    for s in range(3):
        out_ref[s] = total[:, s * 64 : (s + 1) * 64]
    for copy in sent:
        copy.wait_send()


def local(vectors, phi_val, phi_con, screened, partner):
    anyspace = pl.BlockSpec(memory_space=pltpu.HBM)
    dma = pltpu.SemaphoreType.DMA
    out = pl.pallas_call(
        kernel,
        out_shape=jax.ShapeDtypeStruct((3, 8, 64), F32),
        in_specs=[anyspace] * 4,
        out_specs=pl.BlockSpec(memory_space=pltpu.VMEM),
        scratch_shapes=[
            pltpu.VMEM((3, 1, 512), F32),
            pltpu.VMEM((8, 256), F32),
            pltpu.VMEM((8, 8, 256), BF16),
            pltpu.VMEM((4, 8, 8, 256), BF16),
            pltpu.VMEM((2, 4, 64, 256), BF16),
            pltpu.VMEM((4, 2, 4, 64, 256), BF16),
            pltpu.VMEM((64, 256), BF16),
            pltpu.VMEM((4, 64, 256), BF16),
            pltpu.VMEM((4, 256, 2048), BF16),
            pltpu.VMEM((4, 768, 64), BF16),
            pltpu.VMEM((4, 256, 64), BF16),
            pltpu.VMEM((768, 256), F32),
            pltpu.VMEM((768, 256), BF16),
            pltpu.VMEM((64, 768), F32),
            pltpu.VMEM((192, 256), BF16),
            pltpu.VMEM((8, 8, 256), BF16),
            pltpu.VMEM((8, 8, 256), BF16),
            dma((7,)),
            dma((88,)),
            dma((8,)),
            dma((4, 8)),
            dma((4,)),
            dma((4,)),
            dma((4,)),
            dma((2, 4, 4)),
            dma((8,)),
        ],
        compiler_params=pltpu.CompilerParams(collective_id=0, has_side_effects=True, vmem_limit_bytes=32 * 1024 * 1024),
        name="isdf_direct",
    )(*(pltpu.with_memory_space_constraint(a, pltpu.HBM) for a in (vectors, phi_val, phi_con, screened)))
    return out.reshape(3, 1, 512)


def solution(mesh):
    placed = (
        P(None, "ka", "mu"),
        P("ka", None, "mu"),
        P("ka", None, "mu"),
        P(None, "mu", None),
        P("ka", None),
    )
    return jax.shard_map(
        local, mesh=mesh, in_specs=placed, out_specs=P(None, "ka", "mu"), check_vma=False
    )
```

```python
import functools

import jax
import jax.numpy as jnp
from jax import lax
from jax.experimental import pallas as pl
from jax.experimental.pallas import tpu as pltpu
from jax.sharding import PartitionSpec as P

MESH = pl.DeviceIdType.MESH
STEPS = (1, -1, 2, -2)
F32 = jnp.float32
BF16 = jnp.bfloat16


def kernel(
    vec_hbm, val_hbm, con_hbm, scr_hbm, out_ref,
    vec, xbuf, xall, xpart, con_own, con_part, val_own, val_part, scr, yv, val_t, acc, wsum, foldt, fcat, rbuf, rin,
    load_sem, send_sem, rx, rxp, rval, rnear, rfar, rp, rout,
):
    nk = lax.axis_size("ka")
    nmu = lax.axis_size("mu")
    k = lax.axis_index("ka")
    mu = lax.axis_index("mu")
    y, zh = mu // 2, mu % 2

    def wrapped(s):
        whole = (k + s + nk) // nk
        return whole - 1 if s > 0 else 1 - whole

    def ka_of(s):
        return lax.rem(k + s + nk, nk)

    loads = [
        pltpu.make_async_copy(vec_hbm, vec, load_sem.at[0]),
        pltpu.make_async_copy(con_hbm.at[0], con_own.at[zh, y], load_sem.at[1]),
        pltpu.make_async_copy(val_hbm.at[0], val_own, load_sem.at[2]),
    ] + [pltpu.make_async_copy(scr_hbm.at[o], scr.at[o], load_sem.at[3 + o]) for o in range(4)]

    barrier = pltpu.get_barrier_semaphore()
    def greet(device):
        pl.semaphore_signal(barrier, inc=1, device_id=device, device_id_type=MESH)

    def near_half(s):
        return lax.rem(zh + wrapped(s), 2)

    greet({"mu": 2 * y + 1 - zh})
    for d in range(1, 4):
        greet({"mu": 2 * lax.rem(y + d, 4) + zh})
    for s in STEPS:
        greet({"ka": ka_of(s)})
        for yy in range(4):
            greet({"ka": ka_of(s), "mu": 2 * yy + near_half(s)})
    for load in loads:
        load.start()
    loads[0].wait()
    xbuf[...] = jnp.zeros_like(xbuf)
    for s in range(3):
        for r in range(8):
            xbuf[r : r + 1, s * 64 : (s + 1) * 64] = vec[s, :, r * 64 : (r + 1) * 64]
    xall[mu] = xbuf[...].astype(BF16)
    rbuf[...] = jnp.zeros_like(rbuf)
    loads[1].wait()
    loads[2].wait()
    pl.semaphore_wait(barrier, 24)

    sent = []

    def send(src, dst, recv, device):
        copy = pltpu.make_async_remote_copy(
            src_ref=src, dst_ref=dst, send_sem=send_sem.at[len(sent)], recv_sem=recv,
            device_id=device, device_id_type=MESH,
        )
        copy.start()
        sent.append(copy)

    def arrived(ref, recv):
        pltpu.make_async_remote_copy(
            src_ref=ref, dst_ref=ref, send_sem=send_sem.at[0], recv_sem=recv,
            device_id={"mu": lax.rem(mu + 1, nmu)}, device_id_type=MESH,
        ).wait_recv()

    def to_partners_near(yy):
        for o, s in enumerate(STEPS):
            src = con_own.at[zh, yy]
            send(src, con_part.at[o, zh, yy], rp.at[0, o, yy], {"ka": ka_of(s)})

    def to_partners_far(yy):
        for o, s in enumerate(STEPS):
            w = wrapped(s)
            half = lax.rem(zh + 1 + w, 2)
            send(
                con_own.at[half, yy], con_part.at[o, half, yy], rp.at[1, o, yy],
                {"ka": ka_of(s), "mu": 2 * y + lax.rem(zh + w, 2)},
            )

    zo = 1 - zh
    def x_to_partners(m):
        for d in (2, 1, 3, 0):
            for o, s in enumerate(STEPS):
                send(
                    xall.at[m], xpart.at[o, m], rxp.at[o, m],
                    {"ka": ka_of(s), "mu": 2 * lax.rem(y + d, 4) + near_half(s)},
                )

    send(xall.at[mu], xall.at[mu], rx.at[mu], {"mu": 2 * y + zo})
    send(con_own.at[zh, y], con_own.at[zh, y], rfar.at[y], {"mu": 2 * y + zo})
    for d in range(1, 4):
        send(con_own.at[zh, y], con_own.at[zh, y], rnear.at[y], {"mu": 2 * lax.rem(y + d, 4) + zh})
    for o, s in enumerate(STEPS):
        send(val_own, val_part.at[o], rval.at[o], {"ka": ka_of(s)})
    to_partners_near(y)
    for d in (1, 3, 2):
        yy = lax.rem(y + d, 4)
        arrived(con_own.at[zh, yy], rnear.at[yy])
        to_partners_near(yy)
    x_to_partners(mu)
    far = 2 * y + zo
    arrived(xall.at[far], rx.at[far])
    x_to_partners(far)
    arrived(con_own.at[zo, y], rfar.at[y])
    for d in (2, 1, 3):
        send(con_own.at[zo, y], con_own.at[zo, y], rfar.at[y], {"mu": 2 * lax.rem(y + d, 4) + zh})
    for o in range(4):
        arrived(val_part.at[o], rval.at[o])
        val_t[o] = val_part[o].astype(F32).T.astype(BF16)
    foldt[...] = jnp.zeros_like(foldt)
    for d in (1, 3, 2):
        yy = lax.rem(y + d, 4)
        arrived(con_own.at[zo, yy], rfar.at[yy])
        if d == 1:
            to_partners_far(y)
        to_partners_far(yy)

    for o in range(4):
        for m in range(8):
            arrived(xpart.at[o, m], rxp.at[o, m])
        x = xpart[o].astype(F32).reshape(64, 256).astype(BF16)
        mixed = jnp.dot(val_t[o], x, preferred_element_type=F32).astype(BF16)
        for s in range(3):
            yv[o, s * 256 : (s + 1) * 256, :] = mixed[:, s * 64 : (s + 1) * 64]
    for load in loads[3:]:
        load.wait()

    def block(i, carry):
        phase = i // 4
        half = lax.rem(zh + phase, 2)
        turn = lax.rem(i, 4)
        yy = lax.rem(y + turn + (turn // 2) * (1 - 2 * (turn % 2)), 4)
        for o in range(4):
            arrived(con_part.at[o, half, yy], rp.at[phase, o, yy])
        columns = pl.ds(pl.multiple_of((2 * yy + half) * 256, 256), 256)
        for o in range(4):
            weight = scr[o, :, columns].astype(F32)
            for s in range(3):
                rows = slice(s * 256, (s + 1) * 256)
                term = weight * jnp.dot(yv[o, rows, :], con_part[o, half, yy], preferred_element_type=F32)
                if o == 0:
                    acc[rows, :] = term
                elif o < 3:
                    acc[rows, :] += term
                else:
                    wsum[rows, :] = (acc[rows, :] + term).astype(BF16)
        foldt[...] += lax.dot_general(
            con_own[half, yy], wsum[...], (((1,), (1,)), ((), ())), preferred_element_type=F32
        )
        return carry

    lax.fori_loop(0, 8, block, 0)

    for s in range(3):
        fcat[s * 64 : (s + 1) * 64, :] = foldt[:, s * 256 : (s + 1) * 256].astype(BF16)
    result = lax.dot_general(
        val_own[...], fcat[...], (((1,), (1,)), ((), ())), preferred_element_type=F32
    )
    for j in range(8):
        rbuf[j, :, 0:192] = result[j * 8 : (j + 1) * 8, :].astype(BF16)
    before = len(sent)
    for d in (2, 1, 3, 0):
        peer = 2 * lax.rem(y + d, 4) + zo
        send(rbuf.at[peer], rin.at[mu], rout.at[mu], {"mu": peer})
    for d in (2, 1, 3):
        peer = 2 * lax.rem(y + d, 4) + zh
        send(rbuf.at[peer], rin.at[mu], rout.at[mu], {"mu": peer})
    for copy in sent[:before]:
        copy.wait_send()
    total = rbuf[mu].astype(F32)
    for half in (zh, zo):
        for d in (1, 3, 2, 0):
            if d == 0 and half is zh:
                continue
            peer = 2 * lax.rem(y + d, 4) + half
            arrived(rin.at[peer], rout.at[peer])
            total = total + rin[peer].astype(F32)
    for s in range(3):
        out_ref[s] = total[:, s * 64 : (s + 1) * 64]
    for copy in sent[before:]:
        copy.wait_send()


def local(vectors, phi_val, phi_con, screened, partner):
    anyspace = pl.BlockSpec(memory_space=pltpu.HBM)
    dma = pltpu.SemaphoreType.DMA
    out = pl.pallas_call(
        kernel,
        out_shape=jax.ShapeDtypeStruct((3, 8, 64), F32),
        in_specs=[anyspace] * 4,
        out_specs=pl.BlockSpec(memory_space=pltpu.VMEM),
        scratch_shapes=[
            pltpu.VMEM((3, 1, 512), F32),
            pltpu.VMEM((8, 256), F32),
            pltpu.VMEM((8, 8, 256), BF16),
            pltpu.VMEM((4, 8, 8, 256), BF16),
            pltpu.VMEM((2, 4, 64, 256), BF16),
            pltpu.VMEM((4, 2, 4, 64, 256), BF16),
            pltpu.VMEM((64, 256), BF16),
            pltpu.VMEM((4, 64, 256), BF16),
            pltpu.VMEM((4, 256, 2048), BF16),
            pltpu.VMEM((4, 768, 64), BF16),
            pltpu.VMEM((4, 256, 64), BF16),
            pltpu.VMEM((768, 256), F32),
            pltpu.VMEM((768, 256), BF16),
            pltpu.VMEM((64, 768), F32),
            pltpu.VMEM((192, 256), BF16),
            pltpu.VMEM((8, 8, 256), BF16),
            pltpu.VMEM((8, 8, 256), BF16),
            dma((7,)),
            dma((88,)),
            dma((8,)),
            dma((4, 8)),
            dma((4,)),
            dma((4,)),
            dma((4,)),
            dma((2, 4, 4)),
            dma((8,)),
        ],
        compiler_params=pltpu.CompilerParams(collective_id=0, has_side_effects=True, vmem_limit_bytes=32 * 1024 * 1024),
        name="isdf_direct",
    )(*(pltpu.with_memory_space_constraint(a, pltpu.HBM) for a in (vectors, phi_val, phi_con, screened)))
    return out.reshape(3, 1, 512)


def solution(mesh):
    placed = (
        P(None, "ka", "mu"),
        P("ka", None, "mu"),
        P("ka", None, "mu"),
        P(None, "mu", None),
        P("ka", None),
    )
    return jax.shard_map(
        local, mesh=mesh, in_specs=placed, out_specs=P(None, "ka", "mu"), check_vma=False
    )
```

```python
import functools

import jax
import jax.numpy as jnp
from jax import lax
from jax.experimental import pallas as pl
from jax.experimental.pallas import tpu as pltpu
from jax.sharding import PartitionSpec as P

MESH = pl.DeviceIdType.MESH
STEPS = (1, -1, 2, -2)
F32 = jnp.float32
BF16 = jnp.bfloat16


def kernel(
    vec_hbm, val_hbm, con_hbm, scr_hbm, out_ref,
    vec, xbuf, xall, xpart, con_own, con_part, val_own, val_part, scr, yv, val_t, acc, wsum, foldt, fcat, rbuf, rin,
    load_sem, send_sem, rx, rxp, rval, rnear, rfar, rp, rout,
):
    nk = lax.axis_size("ka")
    nmu = lax.axis_size("mu")
    k = lax.axis_index("ka")
    mu = lax.axis_index("mu")
    y, zh = mu // 2, mu % 2

    def wrapped(s):
        whole = (k + s + nk) // nk
        return whole - 1 if s > 0 else 1 - whole

    def ka_of(s):
        return lax.rem(k + s + nk, nk)

    loads = [
        pltpu.make_async_copy(vec_hbm, vec, load_sem.at[0]),
        pltpu.make_async_copy(con_hbm.at[0], con_own.at[zh, y], load_sem.at[1]),
        pltpu.make_async_copy(val_hbm.at[0], val_own, load_sem.at[2]),
    ] + [pltpu.make_async_copy(scr_hbm.at[o], scr.at[o], load_sem.at[3 + o]) for o in range(4)]

    barrier = pltpu.get_barrier_semaphore()
    def greet(device):
        pl.semaphore_signal(barrier, inc=1, device_id=device, device_id_type=MESH)

    def near_half(s):
        return lax.rem(zh + wrapped(s), 2)

    greet({"mu": 2 * y + 1 - zh})
    for d in range(1, 4):
        greet({"mu": 2 * lax.rem(y + d, 4) + zh})
    for s in STEPS:
        greet({"ka": ka_of(s)})
        for yy in range(4):
            greet({"ka": ka_of(s), "mu": 2 * yy + near_half(s)})
    for load in loads:
        load.start()
    loads[0].wait()
    xbuf[...] = jnp.zeros_like(xbuf)
    for s in range(3):
        for r in range(8):
            xbuf[r : r + 1, s * 64 : (s + 1) * 64] = vec[s, :, r * 64 : (r + 1) * 64]
    xall[mu] = xbuf[...].astype(BF16)
    rbuf[...] = jnp.zeros_like(rbuf)
    loads[1].wait()
    loads[2].wait()
    pl.semaphore_wait(barrier, 24)

    sent = []

    def send(src, dst, recv, device):
        copy = pltpu.make_async_remote_copy(
            src_ref=src, dst_ref=dst, send_sem=send_sem.at[len(sent)], recv_sem=recv,
            device_id=device, device_id_type=MESH,
        )
        copy.start()
        sent.append(copy)

    def arrived(ref, recv):
        pltpu.make_async_remote_copy(
            src_ref=ref, dst_ref=ref, send_sem=send_sem.at[0], recv_sem=recv,
            device_id={"mu": lax.rem(mu + 1, nmu)}, device_id_type=MESH,
        ).wait_recv()

    def to_partners_near(yy):
        for o, s in enumerate(STEPS):
            src = con_own.at[zh, yy]
            send(src, con_part.at[o, zh, yy], rp.at[0, o, yy], {"ka": ka_of(s)})

    def to_partners_far(yy):
        for o, s in enumerate(STEPS):
            w = wrapped(s)
            half = lax.rem(zh + 1 + w, 2)
            send(
                con_own.at[half, yy], con_part.at[o, half, yy], rp.at[1, o, yy],
                {"ka": ka_of(s), "mu": 2 * y + lax.rem(zh + w, 2)},
            )

    zo = 1 - zh
    def x_to_partners(m):
        for d in (2, 1, 3, 0):
            for o, s in enumerate(STEPS):
                send(
                    xall.at[m], xpart.at[o, m], rxp.at[o, m],
                    {"ka": ka_of(s), "mu": 2 * lax.rem(y + d, 4) + near_half(s)},
                )

    send(xall.at[mu], xall.at[mu], rx.at[mu], {"mu": 2 * y + zo})
    send(con_own.at[zh, y], con_own.at[zh, y], rfar.at[y], {"mu": 2 * y + zo})
    for d in range(1, 4):
        send(con_own.at[zh, y], con_own.at[zh, y], rnear.at[y], {"mu": 2 * lax.rem(y + d, 4) + zh})
    for o, s in enumerate(STEPS):
        send(val_own, val_part.at[o], rval.at[o], {"ka": ka_of(s)})
    to_partners_near(y)
    for d in (1, 3, 2):
        yy = lax.rem(y + d, 4)
        arrived(con_own.at[zh, yy], rnear.at[yy])
        to_partners_near(yy)
    x_to_partners(mu)
    foldt[...] = jnp.zeros_like(foldt)
    for load in loads[3:]:
        load.wait()
    far = 2 * y + zo
    arrived(xall.at[far], rx.at[far])
    x_to_partners(far)
    arrived(con_own.at[zo, y], rfar.at[y])
    for d in (2, 1, 3):
        send(con_own.at[zo, y], con_own.at[zo, y], rfar.at[y], {"mu": 2 * lax.rem(y + d, 4) + zh})
    for o in range(4):
        arrived(val_part.at[o], rval.at[o])
        val_t[o] = val_part[o].astype(F32).T.astype(BF16)
    for d in (1, 3, 2):
        yy = lax.rem(y + d, 4)
        arrived(con_own.at[zo, yy], rfar.at[yy])
        if d == 1:
            to_partners_far(y)
        to_partners_far(yy)

    for o in range(4):
        for m in range(8):
            arrived(xpart.at[o, m], rxp.at[o, m])
        x = xpart[o].astype(F32).reshape(64, 256).astype(BF16)
        mixed = jnp.dot(val_t[o], x, preferred_element_type=F32).astype(BF16)
        for s in range(3):
            yv[o, s * 256 : (s + 1) * 256, :] = mixed[:, s * 64 : (s + 1) * 64]

    def block(i, carry):
        phase = i // 4
        half = lax.rem(zh + phase, 2)
        turn = lax.rem(i, 4)
        yy = lax.rem(y + turn + (turn // 2) * (1 - 2 * (turn % 2)), 4)
        for o in range(4):
            arrived(con_part.at[o, half, yy], rp.at[phase, o, yy])
        columns = pl.ds(pl.multiple_of((2 * yy + half) * 256, 256), 256)
        for o in range(4):
            weight = scr[o, :, columns].astype(F32)
            for s in range(3):
                rows = slice(s * 256, (s + 1) * 256)
                term = weight * jnp.dot(yv[o, rows, :], con_part[o, half, yy], preferred_element_type=F32)
                if o == 0:
                    acc[rows, :] = term
                elif o < 3:
                    acc[rows, :] += term
                else:
                    wsum[rows, :] = (acc[rows, :] + term).astype(BF16)
        foldt[...] += lax.dot_general(
            con_own[half, yy], wsum[...], (((1,), (1,)), ((), ())), preferred_element_type=F32
        )
        return carry

    lax.fori_loop(0, 8, block, 0)

    for s in range(3):
        fcat[s * 64 : (s + 1) * 64, :] = foldt[:, s * 256 : (s + 1) * 256].astype(BF16)
    result = lax.dot_general(
        val_own[...], fcat[...], (((1,), (1,)), ((), ())), preferred_element_type=F32
    )
    for j in range(8):
        rbuf[j, :, 0:192] = result[j * 8 : (j + 1) * 8, :].astype(BF16)
    before = len(sent)
    for d in (2, 1, 3, 0):
        peer = 2 * lax.rem(y + d, 4) + zo
        send(rbuf.at[peer], rin.at[mu], rout.at[mu], {"mu": peer})
    for d in (2, 1, 3):
        peer = 2 * lax.rem(y + d, 4) + zh
        send(rbuf.at[peer], rin.at[mu], rout.at[mu], {"mu": peer})
    for copy in sent[:before]:
        copy.wait_send()
    total = rbuf[mu].astype(F32)
    for half in (zh, zo):
        for d in (1, 3, 2, 0):
            if d == 0 and half is zh:
                continue
            peer = 2 * lax.rem(y + d, 4) + half
            arrived(rin.at[peer], rout.at[peer])
            total = total + rin[peer].astype(F32)
    for s in range(3):
        out_ref[s] = total[:, s * 64 : (s + 1) * 64]
    for copy in sent[before:]:
        copy.wait_send()


def local(vectors, phi_val, phi_con, screened, partner):
    anyspace = pl.BlockSpec(memory_space=pltpu.HBM)
    dma = pltpu.SemaphoreType.DMA
    out = pl.pallas_call(
        kernel,
        out_shape=jax.ShapeDtypeStruct((3, 8, 64), F32),
        in_specs=[anyspace] * 4,
        out_specs=pl.BlockSpec(memory_space=pltpu.VMEM),
        scratch_shapes=[
            pltpu.VMEM((3, 1, 512), F32),
            pltpu.VMEM((8, 256), F32),
            pltpu.VMEM((8, 8, 256), BF16),
            pltpu.VMEM((4, 8, 8, 256), BF16),
            pltpu.VMEM((2, 4, 64, 256), BF16),
            pltpu.VMEM((4, 2, 4, 64, 256), BF16),
            pltpu.VMEM((64, 256), BF16),
            pltpu.VMEM((4, 64, 256), BF16),
            pltpu.VMEM((4, 256, 2048), BF16),
            pltpu.VMEM((4, 768, 64), BF16),
            pltpu.VMEM((4, 256, 64), BF16),
            pltpu.VMEM((768, 256), F32),
            pltpu.VMEM((768, 256), BF16),
            pltpu.VMEM((64, 768), F32),
            pltpu.VMEM((192, 256), BF16),
            pltpu.VMEM((8, 8, 256), BF16),
            pltpu.VMEM((8, 8, 256), BF16),
            dma((7,)),
            dma((88,)),
            dma((8,)),
            dma((4, 8)),
            dma((4,)),
            dma((4,)),
            dma((4,)),
            dma((2, 4, 4)),
            dma((8,)),
        ],
        compiler_params=pltpu.CompilerParams(collective_id=0, has_side_effects=True, vmem_limit_bytes=32 * 1024 * 1024),
        name="isdf_direct",
    )(*(pltpu.with_memory_space_constraint(a, pltpu.HBM) for a in (vectors, phi_val, phi_con, screened)))
    return out.reshape(3, 1, 512)


def solution(mesh):
    placed = (
        P(None, "ka", "mu"),
        P("ka", None, "mu"),
        P("ka", None, "mu"),
        P(None, "mu", None),
        P("ka", None),
    )
    return jax.shard_map(
        local, mesh=mesh, in_specs=placed, out_specs=P(None, "ka", "mu"), check_vma=False
    )
```
